32 devices in a mesh: pitch: 4 (over x, core), span: 8 (over z, y).
Axes of the slice: x: 2, y: 2, z: 4, core: 2. Of those that a mesh axis runs over, the one named last changes fastest.
Arguments:
- residual: float32 [5, 4, 64, 1024], P(None, None, 'span', 'pitch'), may hold values from -0.6 to 0.6
- inverse_diagonal: float32 [5, 5, 4, 64, 1024], P(None, None, None, 'span', 'pitch'), may hold values from -0.1 to 1, as said below
- prior_increment: float32 [5, 4, 64, 1024], P(None, None, 'span', 'pitch'), may hold values from -3 to 3
- coupling: float32 [6, 5, 5], replicated, may hold values from -1 to 1
- characteristic: float32 [2, 2, 512, 5, 5], replicated, may hold values from -6 to 6
- cutoffs: int32 [2], replicated, may hold values from 128 to 512
Outputs:
- update: float32 [5, 4, 64, 1024], P(None, None, 'span', 'pitch')
The draws below stay inside these ranges and needn't reach their ends.
Inputs may be any that keep to these rules, and one draw needn't show every extreme that they name: `inverse_diagonal`: each cell's block is dominated by its diagonal; the sweeps' recurrences are stable.
All inputs are finite; a program needn't handle non-finite values.
Results may differ from the reference program's by a relative error of at most 0.0003.
Values sent between devices are 32-bit elements; how exact they have to be, the bound alone decides.
A program may use at most 64 MiB of HBM per device.

```python
import jax
import jax.numpy as jnp
from jax import lax

VARIABLES = 5
NP = 1024
HARMONICS = 512
AXIAL = 4
SPANWISE_VOLUMES = 64


def draw_inverse_diagonal(key, part):
    first_key, interaction_seed, third_key = jax.random.split(jax.random.fold_in(key, 11), 3)
    shape = (VARIABLES, AXIAL, SPANWISE_VOLUMES, NP)
    spread = jax.random.uniform(first_key, shape, jnp.float32, 0.0, 0.004)
    relaxation_passes = jax.random.randint(interaction_seed, (2,), 0, SPANWISE_VOLUMES)
    spanwise_location = jnp.arange(SPANWISE_VOLUMES, dtype=jnp.int32)
    affected_volumes = jnp.any(spanwise_location[:, None] == relaxation_passes[None, :], axis=1)
    factor = jnp.where(affected_volumes, 0.75, 1.0).astype(jnp.float32)[None, None, :, None]
    diagonal = jnp.exp(-spread) * factor
    full_shape = (VARIABLES, VARIABLES, AXIAL, SPANWISE_VOLUMES, NP)
    offdiag = jnp.clip(0.03 * jax.random.normal(third_key, full_shape, jnp.float32), -0.1, 0.1)
    identity = jnp.eye(VARIABLES, dtype=jnp.float32)[:, :, None, None, None]
    return offdiag * (1.0 - identity) + identity * diagonal[:, None]


def draw_coupling(key, part):
    keys = jax.random.split(jax.random.fold_in(key, 23), 4)
    order = jax.random.permutation(keys[0], VARIABLES)
    slow = order < 3
    rates = jnp.where(slow, 0.998, 0.9).astype(jnp.float32)
    lower_part = jnp.tril(0.05 * jax.random.normal(keys[1], (VARIABLES, VARIABLES), jnp.float32), -1)
    upper_part = jnp.tril(0.05 * jax.random.normal(keys[2], (VARIABLES, VARIABLES), jnp.float32), -1)
    radial_lower = -(jnp.diag(rates) + lower_part)
    radial_upper = jnp.diag(rates) + upper_part
    others = jnp.clip(0.1 * jax.random.normal(keys[3], (4, VARIABLES, VARIABLES), jnp.float32), -0.4, 0.4)
    return jnp.concatenate([radial_lower[None], radial_upper[None], others], axis=0)


def block_scale(rng, shape, pieces, low, high):
    def one(position, parts):
        steps = jax.random.uniform(jax.random.fold_in(jax.random.fold_in(rng, 6), position), (parts,), jnp.float32, low / len(pieces), high / len(pieces))
        return jnp.repeat(jnp.exp(steps), shape[position] // parts).reshape((-1,) + (1,) * (len(shape) - position - 1))

    gain = one(*pieces[0])
    for cut in pieces[1:]:
        gain = gain * one(*cut)
    return gain


def bell_draw(rng, extent, deviation, limit, cuts=(), kind=jnp.bfloat16):
    loudness = block_scale(rng, extent, cuts, -0.22, 0.18) if cuts else 1.0
    values = jax.random.normal(rng, extent, jnp.float32) * deviation * loudness
    return jnp.minimum(jnp.maximum(values, -limit), limit).astype(kind)


def setup_inputs(seed: int = 0) -> dict:
    streams_of = jax.random.split(jax.random.key(seed), 7)
    residual = bell_draw(streams_of[0], (VARIABLES, AXIAL, SPANWISE_VOLUMES, NP), 0.1, 0.6, ((2, 8), (3, 4)), jnp.float32)
    inverse_diagonal = draw_inverse_diagonal(jax.random.fold_in(streams_of[6], 71), 0)
    prior_increment = bell_draw(streams_of[2], (VARIABLES, AXIAL, SPANWISE_VOLUMES, NP), 0.5, 3.0, ((2, 8), (3, 4)), jnp.float32)
    coupling = draw_coupling(jax.random.fold_in(streams_of[6], 71), 0)
    characteristic = bell_draw(streams_of[4], (2, 2, HARMONICS, VARIABLES, VARIABLES), 1.0, 6.0, (), jnp.float32)
    cutoffs = jax.random.randint(streams_of[5], (2,), HARMONICS // 4, HARMONICS + 1).astype(jnp.int32)
    return {"residual": residual, "inverse_diagonal": inverse_diagonal, "prior_increment": prior_increment, "coupling": coupling, "characteristic": characteristic, "cutoffs": cutoffs}


highest = lax.Precision.HIGHEST


def angle_tables(pitch_index, harmonic_index, points):
    product = (pitch_index[:, None] * harmonic_index[None, :]) % points
    angles = product.astype(jnp.float32) * (2.0 * jnp.pi / points)
    return jnp.cos(angles), jnp.sin(angles)


def forward_dft(spanwise_slices, cosine, sine):
    flat = spanwise_slices.reshape(-1, spanwise_slices.shape[-1])
    shape = spanwise_slices.shape[:-1] + (cosine.shape[1],)
    real_part = jnp.dot(flat, cosine, precision=highest).reshape(shape)
    imag_part = -jnp.dot(flat, sine, precision=highest).reshape(shape)
    return real_part, imag_part


def contract(matrix, spectrum):
    return jnp.einsum('pkij,pjrk->pirk', matrix, spectrum, precision=highest)


def apply_harmonics(real_part, imag_part, characteristic, cutoffs, first_harmonic, points):
    char_real = characteristic[:, 0]
    char_imag = characteristic[:, 1]
    result_real_component = contract(char_real, real_part) - contract(char_imag, imag_part)
    out_imag = contract(char_real, imag_part) + contract(char_imag, real_part)
    harmonic = first_harmonic + jnp.arange(real_part.shape[-1], dtype=jnp.int32)
    kept = (harmonic[None, :] < cutoffs[:, None]).astype(jnp.float32)
    weight = jnp.where(harmonic == 0, 1.0, 2.0).astype(jnp.float32) / points
    factor = (kept * weight[None, :])[:, None, None, :]
    return result_real_component * factor, out_imag * factor


def inverse_dft(result_real_component, out_imag, cosine, sine):
    shape = result_real_component.shape[:-1] + (cosine.shape[0],)
    flat_real = result_real_component.reshape(-1, result_real_component.shape[-1])
    flat_imag = out_imag.reshape(-1, out_imag.shape[-1])
    result = jnp.dot(flat_real, cosine.T, precision=highest) - jnp.dot(flat_imag, sine.T, precision=highest)
    return result.reshape(shape)


def mix_field(matrix, field):
    return jnp.einsum('ij,jarp->iarp', matrix, field, precision=highest)


def mix_vector(matrix, vector):
    return jnp.einsum('ij,jap->iap', matrix, vector, precision=highest)


def apply_block(block, vector):
    return jnp.einsum('ijap,jap->iap', block, vector, precision=highest)


def reference(residual, inverse_diagonal, prior_increment, coupling, characteristic, cutoffs):
    spanwise_slices = jnp.stack([residual[:, 0], residual[:, -1]])
    pitch_index = jnp.arange(NP, dtype=jnp.int32)
    harmonic_index = jnp.arange(HARMONICS, dtype=jnp.int32)
    cosine, sine = angle_tables(pitch_index, harmonic_index, NP)
    real_part, imag_part = forward_dft(spanwise_slices, cosine, sine)
    result_real_component, out_imag = apply_harmonics(real_part, imag_part, characteristic, cutoffs, 0, NP)
    correction = inverse_dft(result_real_component, out_imag, cosine, sine)
    corrected = residual.at[:, 0].add(correction[0]).at[:, -1].add(correction[1])
    padded = jnp.concatenate([prior_increment[..., -1:], prior_increment, prior_increment[..., :1]], axis=3)
    axial_pad = jnp.pad(prior_increment, ((0, 0), (1, 1), (0, 0), (0, 0)))
    source = corrected - mix_field(coupling[2], padded[..., :-2]) - mix_field(coupling[3], padded[..., 2:])
    source = source - mix_field(coupling[4], axial_pad[:, :-2]) - mix_field(coupling[5], axial_pad[:, 2:])
    diag_rows = jnp.moveaxis(inverse_diagonal, 3, 0)
    source_rows = jnp.moveaxis(source, 2, 0)
    zeros = jnp.zeros((residual.shape[0], residual.shape[1], residual.shape[3]), jnp.float32)

    def forward_sweep_step(previous, pair):
        block, rhs_row = pair
        current = apply_block(block, rhs_row - mix_vector(coupling[0], previous))
        return current, current

    _, star_rows = lax.scan(forward_sweep_step, zeros, (diag_rows, source_rows))

    def backward_step(following, pair):
        block, star_row = pair
        current = star_row - apply_block(block, mix_vector(coupling[1], following))
        return current, current

    _, final_rows = lax.scan(backward_step, zeros, (diag_rows, star_rows), reverse=True)
    return jnp.moveaxis(final_rows, 0, 2)
```

```python
import jax
import jax.numpy as jnp
import numpy as np
from jax import lax
from jax.experimental import pallas as pl
from jax.experimental.pallas import tpu as pltpu
from jax.sharding import PartitionSpec as P

highest = lax.Precision.HIGHEST
LANES = 128
VMEM = pltpu.VMEM
SMEM = pltpu.SMEM


def exchange(blocks, axis, gather, collective):
    n = lax.axis_size(axis)
    part = blocks.shape if gather else blocks.shape[1:]

    def kernel(x_ref, o_ref, send, recv, own):
        me = lax.axis_index(axis)
        barrier = pltpu.get_barrier_semaphore()
        for step in range(1, n):
            pl.semaphore_signal(
                barrier,
                inc=1,
                device_id={axis: lax.rem(me + step, n)},
                device_id_type=pl.DeviceIdType.MESH,
            )
        local = pltpu.make_async_copy(x_ref if gather else x_ref.at[me], o_ref.at[me], own)
        local.start()
        pl.semaphore_wait(barrier, n - 1)
        copies = []
        for step in range(1, n):
            to = lax.rem(me + step, n)
            copy = pltpu.make_async_remote_copy(
                src_ref=x_ref if gather else x_ref.at[to],
                dst_ref=o_ref.at[me],
                send_sem=send.at[step - 1],
                recv_sem=recv.at[step - 1],
                device_id={axis: to},
                device_id_type=pl.DeviceIdType.MESH,
            )
            copy.start()
            copies.append(copy)
        local.wait()
        for copy in copies:
            copy.wait()

    return pl.pallas_call(
        kernel,
        out_shape=jax.ShapeDtypeStruct((n,) + part, jnp.float32),
        in_specs=[pl.BlockSpec(memory_space=VMEM)],
        out_specs=pl.BlockSpec(memory_space=VMEM),
        scratch_shapes=[
            pltpu.SemaphoreType.DMA((n - 1,)),
            pltpu.SemaphoreType.DMA((n - 1,)),
            pltpu.SemaphoreType.DMA,
        ],
        compiler_params=pltpu.CompilerParams(collective_id=collective, has_side_effects=True),
        name="exchange_%d" % collective,
    )(blocks)


def total(terms):
    result = terms[0]
    for term in terms[1:]:
        result = result + term
    return result


def scaled(block, matrix, nv):
    return [
        [-total([block[i][j] * matrix(j, k) for j in range(nv)]) for k in range(nv)]
        for i in range(nv)
    ]


def times(block, vector, nv):
    return [total([block[i][j] * vector[j] for j in range(nv)]) for i in range(nv)]


def load_block(diag, row, nv):
    return [[diag[i * nv + j, row] for j in range(nv)] for i in range(nv)]


def local_kernel(nv, coupling, diag, residual, neighbours, source, packed, maps, stars):
    rows = diag.shape[1]
    tile = diag.shape[2:]
    zero = jnp.zeros(tile, jnp.float32)
    one = jnp.ones(tile, jnp.float32)

    def entry(which):
        return lambda i, j: coupling[(which * nv + i) * nv + j]

    identity = [zero + (one if i == j else zero) for j in range(nv) for i in range(nv)]

    def column(flat, j):
        return flat[j * nv:(j + 1) * nv]

    def forward(row, carry):
        star, grown = list(carry[:nv]), list(carry[nv:])
        block = load_block(diag, row, nv)
        rhs = []
        for i in range(nv):
            value = residual[i, row]
            for side in range(4):
                matrix = entry(2 + side)
                for j in range(nv):
                    value = value - matrix(i, j) * neighbours[side * nv + j, row]
            source[i, row] = value
            rhs.append(value)
        step = scaled(block, entry(0), nv)
        star = [x + y for x, y in zip(times(block, rhs, nv), times(step, star, nv))]
        new = []
        for j in range(nv):
            new += times(step, column(grown, j), nv)
        for i in range(nv):
            stars[row, i] = star[i]
        for m in range(nv * nv):
            maps[row, m] = new[m]
        return tuple(star + new)

    last = lax.fori_loop(0, rows, forward, tuple([zero] * nv + identity))
    for m in range(nv + nv * nv):
        packed[m] = last[m]

    def backward(index, carry):
        row = rows - 1 - index
        nn = nv * nv
        base, response, grown = list(carry[:nv]), list(carry[nv:nv + nn]), list(carry[nv + nn:])
        step = scaled(load_block(diag, row, nv), entry(1), nv)
        base = [stars[row, i] + y for i, y in enumerate(times(step, base, nv))]
        new_response, new = [], []
        for j in range(nv):
            moved = times(step, column(response, j), nv)
            new_response += [maps[row, j * nv + i] + moved[i] for i in range(nv)]
            new += times(step, column(grown, j), nv)
        return tuple(base + new_response + new)

    initial = tuple([zero] * (nv + nv * nv) + identity)
    final = lax.fori_loop(0, rows, backward, initial)
    for m in range(nv + 2 * nv * nv):
        packed[nv + nv * nv + m] = final[m]


def solve_kernel(nv, got, out):
    n = got.shape[0]
    lanes = got.shape[2]
    nn = nv * nv

    def mapped(d, start, vector):
        return total(
            [
                got[d, start + j * nv:start + (j + 1) * nv, :] * vector[j:j + 1]
                for j in range(nv)
            ]
        )

    incoming = jnp.zeros((nv, lanes), jnp.float32)
    all_incoming = []
    for d in range(n):
        all_incoming.append(incoming)
        out[d, 0:nv, :] = incoming
        if d + 1 < n:
            incoming = got[d, 0:nv, :] + mapped(d, nv, incoming)
    following = jnp.zeros((nv, lanes), jnp.float32)
    base = nv + nn
    for d in reversed(range(n)):
        out[d, nv:2 * nv, :] = following
        if d > 0:
            known = got[d, base:base + nv, :] + mapped(d, base + nv, all_incoming[d])
            following = known + mapped(d, base + nv + nn, following)


def final_kernel(nv, coupling, diag, source, incoming, update, stars):
    rows = diag.shape[1]

    def mixed(which, vector):
        return [
            total([coupling[(which * nv + i) * nv + j] * vector[j] for j in range(nv)])
            for i in range(nv)
        ]

    def forward(row, star):
        pushed = mixed(0, star)
        rhs = [source[i, row] - pushed[i] for i in range(nv)]
        star = times(load_block(diag, row, nv), rhs, nv)
        for i in range(nv):
            stars[row, i] = star[i]
        return tuple(star)

    lax.fori_loop(0, rows, forward, tuple(incoming[i] for i in range(nv)))

    def backward(index, following):
        row = rows - 1 - index
        moved = times(load_block(diag, row, nv), mixed(1, following), nv)
        value = [stars[row, i] - moved[i] for i in range(nv)]
        for i in range(nv):
            update[i, row] = value[i]
        return tuple(value)

    lax.fori_loop(0, rows, backward, tuple(incoming[nv + i] for i in range(nv)))


def tables(n, width, harmonics):
    points = n * width
    own = harmonics // n
    k = n * np.arange(own)[None, :] + np.arange(n)[:, None]
    product = (np.arange(width)[None, :, None] * k[:, None, :]) % points
    angle = product * (2.0 * np.pi / points)
    return np.stack([np.cos(angle), np.sin(angle)], axis=1).astype(np.float32)


def corrections(residual, prior, characteristic, cutoffs):
    n = lax.axis_size("pitch")
    me = lax.axis_index("pitch")
    nv, _, rows, width = residual.shape
    harmonics = characteristic.shape[2]
    points = n * width
    own = harmonics // n
    flat_rows = 2 * nv * rows
    planes = jnp.stack([residual[:, 0], residual[:, -1]]).reshape(flat_rows, width)
    edges = jnp.stack([prior[..., 0], prior[..., -1]]).reshape(-1)
    edge_rows = -(-edges.shape[0] // width)
    edge_rows = -(-edge_rows // 8) * 8
    edges = jnp.pad(edges, (0, edge_rows * width - edges.shape[0])).reshape(edge_rows, width)
    gathered = exchange(jnp.concatenate([planes, edges]), "pitch", True, 0)

    edge_shape = (2,) + prior.shape[:-1]
    count = int(np.prod(edge_shape))

    def edges_of(device):
        piece = lax.dynamic_index_in_dim(gathered, device, 0, keepdims=False)[flat_rows:]
        return piece.reshape(-1)[:count].reshape(edge_shape)

    before = edges_of(lax.rem(me + n - 1, n))[1][..., None]
    after = edges_of(lax.rem(me + 1, n))[0][..., None]

    turn = 2.0 * np.pi * (np.arange(n)[:, None] * np.arange(n)[None, :] % n) / n
    turn_cos = lax.dynamic_index_in_dim(jnp.asarray(np.cos(turn), jnp.float32), me, 0, keepdims=False)
    turn_sin = lax.dynamic_index_in_dim(jnp.asarray(np.sin(turn), jnp.float32), me, 0, keepdims=False)
    waves = total([gathered[q, :flat_rows] * turn_cos[q] for q in range(n)])
    waves_imag = -total([gathered[q, :flat_rows] * turn_sin[q] for q in range(n)])
    table = lax.dynamic_index_in_dim(jnp.asarray(tables(n, width, harmonics)), me, 0, keepdims=False)
    cosine, sine = table[0], table[1]
    both = jnp.concatenate([waves, waves_imag], axis=1)
    matrix = jnp.concatenate(
        [jnp.concatenate([cosine, -sine], axis=1), jnp.concatenate([sine, cosine], axis=1)]
    )
    spectrum = jnp.dot(both, matrix, precision=highest).reshape(2, nv, rows, 2 * own)
    real_part, imag_part = spectrum[..., :own], spectrum[..., own:]

    mine = n * jnp.arange(own, dtype=jnp.int32) + me
    chosen = (jnp.arange(harmonics, dtype=jnp.int32)[:, None] == mine[None, :]).astype(jnp.float32)
    by_entry = characteristic.transpose(3, 4, 0, 1, 2).reshape(-1, harmonics)
    picked = jnp.dot(by_entry, chosen, precision=highest).reshape(nv, nv, 2, 2, 1, own)
    out_real, out_imag = [], []
    kept = (mine[None, :] < cutoffs[:, None]).astype(jnp.float32)
    weight = jnp.where(mine == 0, 1.0, 2.0).astype(jnp.float32) / points
    factor = (kept * weight[None, :])[:, None, :]
    for i in range(nv):
        cr = [picked[i, j, :, 0] for j in range(nv)]
        ci = [picked[i, j, :, 1] for j in range(nv)]
        out_real.append(
            total([cr[j] * real_part[:, j] - ci[j] * imag_part[:, j] for j in range(nv)]) * factor
        )
        out_imag.append(
            total([cr[j] * imag_part[:, j] + ci[j] * real_part[:, j] for j in range(nv)]) * factor
        )
    corrected = jnp.concatenate(
        [jnp.stack(out_real, axis=1), jnp.stack(out_imag, axis=1)], axis=-1
    ).reshape(flat_rows, 2 * own)
    back = jnp.concatenate(
        [
            jnp.concatenate([cosine.T, sine.T], axis=1),
            jnp.concatenate([-sine.T, cosine.T], axis=1),
        ]
    )
    field = jnp.dot(corrected, back, precision=highest)
    parts = jnp.stack(
        [field[:, :width] * turn_cos[q] - field[:, width:] * turn_sin[q] for q in range(n)]
    )
    received = exchange(parts, "pitch", False, 1)
    correction = received.sum(axis=0).reshape(2, nv, rows, width)
    return correction, before, after


def body(residual, inverse_diagonal, prior, coupling, characteristic, cutoffs):
    nv, axial, rows, width = residual.shape
    cells = axial * width
    tile = (cells // LANES, LANES)
    n = lax.axis_size("span")

    def by_row(field):
        lead = field.shape[:-3]
        return jnp.moveaxis(field, -2, -3).reshape((-1, rows) + tile)

    diag = by_row(inverse_diagonal)
    correction, before, after = corrections(residual, prior, characteristic, cutoffs)
    corrected = by_row(residual.at[:, 0].add(correction[0]).at[:, -1].add(correction[1]))
    blank = jnp.zeros_like(prior[:, :1])
    neighbours = by_row(
        jnp.stack(
            [
                jnp.concatenate([before, prior[..., :-1]], axis=3),
                jnp.concatenate([prior[..., 1:], after], axis=3),
                jnp.concatenate([blank, prior[:, :-1]], axis=1),
                jnp.concatenate([prior[:, 1:], blank], axis=1),
            ]
        )
    )
    scalars = coupling.reshape(-1)
    nn = nv * nv
    count = 2 * nv + 3 * nn
    smem = pl.BlockSpec(memory_space=SMEM)
    vmem = pl.BlockSpec(memory_space=VMEM)
    source, packed = pl.pallas_call(
        lambda *refs: local_kernel(nv, *refs),
        out_shape=(
            jax.ShapeDtypeStruct((nv, rows) + tile, jnp.float32),
            jax.ShapeDtypeStruct((count,) + tile, jnp.float32),
        ),
        in_specs=[smem, vmem, vmem, vmem],
        out_specs=(vmem, vmem),
        scratch_shapes=[
            VMEM((rows, nn) + tile, jnp.float32),
            VMEM((rows, nv) + tile, jnp.float32),
        ],
        name="local_sweeps",
    )(scalars, diag, corrected, neighbours)
    share = cells // n
    blocks = packed.reshape(count, n, share).transpose(1, 0, 2)
    got = exchange(blocks, "span", False, 2)
    solved = pl.pallas_call(
        lambda *refs: solve_kernel(nv, *refs),
        out_shape=jax.ShapeDtypeStruct((n, 2 * nv, share), jnp.float32),
        in_specs=[vmem],
        out_specs=vmem,
        name="solve",
    )(got)
    back = exchange(solved, "span", False, 3)
    incoming = back.transpose(1, 0, 2).reshape((2 * nv,) + tile)
    update = pl.pallas_call(
        lambda *refs: final_kernel(nv, *refs),
        out_shape=jax.ShapeDtypeStruct((nv, rows) + tile, jnp.float32),
        in_specs=[smem, vmem, vmem, vmem],
        out_specs=vmem,
        scratch_shapes=[VMEM((rows, nv) + tile, jnp.float32)],
        name="final_sweeps",
    )(scalars, diag, source, incoming)
    return jnp.moveaxis(update.reshape(nv, rows, axial, width), 1, 2)


def solution(mesh):
    in_specs = (
        P(None, None, "span", "pitch"),
        P(None, None, None, "span", "pitch"),
        P(None, None, "span", "pitch"),
        P(),
        P(),
        P(),
    )
    out_specs = P(None, None, "span", "pitch")
    return jax.shard_map(body, mesh=mesh, in_specs=in_specs, out_specs=out_specs, check_vma=False)
```

```python
import jax
import jax.numpy as jnp
import numpy as np
from jax import lax
from jax.experimental import pallas as pl
from jax.experimental.pallas import tpu as pltpu
from jax.sharding import PartitionSpec as P

highest = lax.Precision.HIGHEST
LANES = 128
VMEM = pltpu.VMEM
SMEM = pltpu.SMEM


def greet(axis):
    n = lax.axis_size(axis)
    me = lax.axis_index(axis)
    barrier = pltpu.get_barrier_semaphore()
    for step in range(1, n):
        pl.semaphore_signal(
            barrier,
            inc=1,
            device_id={axis: lax.rem(me + step, n)},
            device_id_type=pl.DeviceIdType.MESH,
        )


def greeted(axis):
    pl.semaphore_wait(pltpu.get_barrier_semaphore(), lax.axis_size(axis) - 1)


def start_exchange(source, target, send, recv, axis, gather):
    n = lax.axis_size(axis)
    me = lax.axis_index(axis)
    copies = []
    for step in range(1, n):
        to = lax.rem(me + step, n)
        copy = pltpu.make_async_remote_copy(
            src_ref=source if gather else source.at[to],
            dst_ref=target.at[me],
            send_sem=send.at[step - 1],
            recv_sem=recv.at[step - 1],
            device_id={axis: to},
            device_id_type=pl.DeviceIdType.MESH,
        )
        copy.start()
        copies.append(copy)
    return copies


def wait_all(copies):
    for copy in copies:
        copy.wait()


def semaphores(axis, exchanges):
    n = lax.axis_size(axis)
    return [pltpu.SemaphoreType.DMA((n - 1,)) for _ in range(2 * exchanges)]


def total(terms):
    result = terms[0]
    for term in terms[1:]:
        result = result + term
    return result


def scaled(block, matrix, nv):
    return [
        [-total([block[i][j] * matrix(j, k) for j in range(nv)]) for k in range(nv)]
        for i in range(nv)
    ]


def times(block, vector, nv):
    return [total([block[i][j] * vector[j] for j in range(nv)]) for i in range(nv)]


def load_block(diag, row, nv):
    return [[diag[i * nv + j, row] for j in range(nv)] for i in range(nv)]


def local_kernel(nv, coupling, diag, residual, neighbours, source, packed, maps, stars):
    rows = diag.shape[1]
    tile = diag.shape[2:]
    zero = jnp.zeros(tile, jnp.float32)
    one = jnp.ones(tile, jnp.float32)

    def entry(which):
        return lambda i, j: coupling[(which * nv + i) * nv + j]

    identity = [zero + (one if i == j else zero) for j in range(nv) for i in range(nv)]

    def column(flat, j):
        return flat[j * nv:(j + 1) * nv]

    def forward(row, carry):
        star, grown = list(carry[:nv]), list(carry[nv:])
        block = load_block(diag, row, nv)
        rhs = []
        for i in range(nv):
            value = residual[i, row]
            for side in range(4):
                matrix = entry(2 + side)
                for j in range(nv):
                    value = value - matrix(i, j) * neighbours[side * nv + j, row]
            source[i, row] = value
            rhs.append(value)
        step = scaled(block, entry(0), nv)
        star = [x + y for x, y in zip(times(block, rhs, nv), times(step, star, nv))]
        new = []
        for j in range(nv):
            new += times(step, column(grown, j), nv)
        for i in range(nv):
            stars[row, i] = star[i]
        for m in range(nv * nv):
            maps[row, m] = new[m]
        return tuple(star + new)

    last = lax.fori_loop(0, rows, forward, tuple([zero] * nv + identity))
    for m in range(nv + nv * nv):
        packed[m] = last[m]

    def backward(index, carry):
        row = rows - 1 - index
        nn = nv * nv
        base, response, grown = list(carry[:nv]), list(carry[nv:nv + nn]), list(carry[nv + nn:])
        step = scaled(load_block(diag, row, nv), entry(1), nv)
        base = [stars[row, i] + y for i, y in enumerate(times(step, base, nv))]
        new_response, new = [], []
        for j in range(nv):
            moved = times(step, column(response, j), nv)
            new_response += [maps[row, j * nv + i] + moved[i] for i in range(nv)]
            new += times(step, column(grown, j), nv)
        return tuple(base + new_response + new)

    initial = tuple([zero] * (nv + nv * nv) + identity)
    final = lax.fori_loop(0, rows, backward, initial)
    for m in range(nv + 2 * nv * nv):
        packed[nv + nv * nv + m] = final[m]


def solve_kernel(nv, got, out):
    n = got.shape[0]
    lanes = got.shape[2]
    nn = nv * nv

    def mapped(d, start, vector):
        return total(
            [
                got[d, start + j * nv:start + (j + 1) * nv, :] * vector[j:j + 1]
                for j in range(nv)
            ]
        )

    incoming = jnp.zeros((nv, lanes), jnp.float32)
    all_incoming = []
    for d in range(n):
        all_incoming.append(incoming)
        out[d, 0:nv, :] = incoming
        if d + 1 < n:
            incoming = got[d, 0:nv, :] + mapped(d, nv, incoming)
    following = jnp.zeros((nv, lanes), jnp.float32)
    base = nv + nn
    for d in reversed(range(n)):
        out[d, nv:2 * nv, :] = following
        if d > 0:
            known = got[d, base:base + nv, :] + mapped(d, base + nv, all_incoming[d])
            following = known + mapped(d, base + nv + nn, following)


def final_kernel(nv, coupling, diag, source, incoming, update, stars):
    rows = diag.shape[1]

    def mixed(which, vector):
        return [
            total([coupling[(which * nv + i) * nv + j] * vector[j] for j in range(nv)])
            for i in range(nv)
        ]

    def forward(row, star):
        pushed = mixed(0, star)
        rhs = [source[i, row] - pushed[i] for i in range(nv)]
        star = times(load_block(diag, row, nv), rhs, nv)
        for i in range(nv):
            stars[row, i] = star[i]
        return tuple(star)

    lax.fori_loop(0, rows, forward, tuple(incoming[i] for i in range(nv)))

    def backward(index, following):
        row = rows - 1 - index
        moved = times(load_block(diag, row, nv), mixed(1, following), nv)
        value = [stars[row, i] - moved[i] for i in range(nv)]
        for i in range(nv):
            update[i, row] = value[i]
        return tuple(value)

    lax.fori_loop(0, rows, backward, tuple(incoming[nv + i] for i in range(nv)))


def spectral_kernel(
    nv, rows, turn, x_ref, table, picked, factor, out, edges, got, parts, landed, s0, r0, s1, r1
):
    n = lax.axis_size("pitch")
    me = lax.axis_index("pitch")
    flat = 2 * nv * rows
    greet("pitch")
    got[me] = x_ref[...]
    greeted("pitch")
    wait_all(start_exchange(x_ref, got, s0, r0, "pitch", True))
    edges[...] = got[:, flat:, :]
    waves = total([got[q, :flat, :] * turn[q] for q in range(n)])
    waves_imag = -total([got[q, :flat, :] * turn[n + q] for q in range(n)])
    both = jnp.concatenate([waves, waves_imag])
    cosine, sine = table[0], table[1]
    with_cos = jnp.dot(both, cosine, precision=highest, preferred_element_type=jnp.float32)
    with_sin = jnp.dot(both, sine, precision=highest, preferred_element_type=jnp.float32)
    real_part = with_cos[:flat] + with_sin[flat:]
    imag_part = with_cos[flat:] - with_sin[:flat]
    out_real, out_imag = [], []
    for q in range(2):
        weight = factor[q:q + 1, :]
        sr = [real_part[(q * nv + j) * rows:(q * nv + j + 1) * rows] for j in range(nv)]
        si = [imag_part[(q * nv + j) * rows:(q * nv + j + 1) * rows] for j in range(nv)]
        for i in range(nv):
            at = [((i * nv + j) * 2 + q) * 2 for j in range(nv)]
            cr = [picked[m:m + 1, :] for m in at]
            ci = [picked[m + 1:m + 2, :] for m in at]
            out_real.append(total([cr[j] * sr[j] - ci[j] * si[j] for j in range(nv)]) * weight)
            out_imag.append(total([cr[j] * si[j] + ci[j] * sr[j] for j in range(nv)]) * weight)
    stacked = jnp.concatenate(out_real + out_imag)

    def back(matrix):
        return lax.dot_general(
            stacked,
            matrix,
            (((1,), (1,)), ((), ())),
            precision=highest,
            preferred_element_type=jnp.float32,
        )

    with_cos, with_sin = back(cosine), back(sine)
    field = with_cos[:flat] - with_sin[flat:]
    field_imag = with_sin[:flat] + with_cos[flat:]
    for q in range(n):
        parts[q] = field * turn[q] - field_imag * turn[n + q]
    copies = start_exchange(parts, landed, s1, r1, "pitch", False)
    landed[me] = parts[me]
    wait_all(copies)
    out[...] = total([landed[q] for q in range(n)])


def sweeps_kernel(
    nv, coupling, diag, residual, neighbours, update,
    source, maps, stars, packed, send, got, solved, back, incoming, s0, r0, s1, r1
):
    n = lax.axis_size("span")
    me = lax.axis_index("span")
    share = send.shape[2]
    pieces = LANES // share
    greet("span")
    local_kernel(nv, coupling, diag, residual, neighbours, source, packed, maps, stars)
    for m in range(packed.shape[0]):
        value = packed[m]
        if pieces == 1:
            send[:, m, :] = value
        else:
            for d in range(n):
                lane = d % pieces * share
                row = d // pieces
                send[d, m:m + 1, :] = value[row:row + 1, lane:lane + share]
    greeted("span")
    copies = start_exchange(send, got, s0, r0, "span", False)
    got[me] = send[me]
    wait_all(copies)
    solve_kernel(nv, got, solved)
    copies = start_exchange(solved, back, s1, r1, "span", False)
    back[me] = solved[me]
    wait_all(copies)
    for m in range(2 * nv):
        if pieces == 1:
            incoming[m] = back[:, m, :]
        else:
            for d in range(n):
                lane = d % pieces * share
                row = d // pieces
                incoming[m, row:row + 1, lane:lane + share] = back[d, m:m + 1, :]
    final_kernel(nv, coupling, diag, source, incoming, update, stars)


def tables(n, width, harmonics):
    points = n * width
    own = harmonics // n
    k = n * np.arange(own)[None, :] + np.arange(n)[:, None]
    product = (np.arange(width)[None, :, None] * k[:, None, :]) % points
    angle = product * (2.0 * np.pi / points)
    return np.stack([np.cos(angle), np.sin(angle)], axis=1).astype(np.float32)


def corrections(residual, prior, characteristic, cutoffs):
    n = lax.axis_size("pitch")
    me = lax.axis_index("pitch")
    nv, _, rows, width = residual.shape
    harmonics = characteristic.shape[2]
    points = n * width
    own = harmonics // n
    flat_rows = 2 * nv * rows
    planes = jnp.stack([residual[:, 0], residual[:, -1]]).reshape(flat_rows, width)
    edges = jnp.stack([prior[..., 0], prior[..., -1]]).reshape(-1)
    edge_rows = -(-edges.shape[0] // width)
    edge_rows = -(-edge_rows // 8) * 8
    edges = jnp.pad(edges, (0, edge_rows * width - edges.shape[0])).reshape(edge_rows, width)
    turn = 2.0 * np.pi * (np.arange(n)[:, None] * np.arange(n)[None, :] % n) / n
    turn_cos = lax.dynamic_index_in_dim(jnp.asarray(np.cos(turn), jnp.float32), me, 0, keepdims=False)
    turn_sin = lax.dynamic_index_in_dim(jnp.asarray(np.sin(turn), jnp.float32), me, 0, keepdims=False)
    table = lax.dynamic_index_in_dim(jnp.asarray(tables(n, width, harmonics)), me, 0, keepdims=False)
    mine = n * jnp.arange(own, dtype=jnp.int32) + me
    chosen = (jnp.arange(harmonics, dtype=jnp.int32)[:, None] == mine[None, :]).astype(jnp.float32)
    by_entry = characteristic.transpose(3, 4, 0, 1, 2).reshape(-1, harmonics)
    picked = jnp.dot(by_entry, chosen, precision=highest)
    kept = (mine[None, :] < cutoffs[:, None]).astype(jnp.float32)
    weight = jnp.where(mine == 0, 1.0, 2.0).astype(jnp.float32) / points
    factor = kept * weight[None, :]
    smem = pl.BlockSpec(memory_space=SMEM)
    vmem = pl.BlockSpec(memory_space=VMEM)
    total_rows = flat_rows + edge_rows
    correction, gathered = pl.pallas_call(
        lambda *refs: spectral_kernel(nv, rows, *refs),
        out_shape=(
            jax.ShapeDtypeStruct((flat_rows, width), jnp.float32),
            jax.ShapeDtypeStruct((n, edge_rows, width), jnp.float32),
        ),
        in_specs=[smem, vmem, vmem, vmem, vmem],
        out_specs=(vmem, vmem),
        scratch_shapes=[
            VMEM((n, total_rows, width), jnp.float32),
            VMEM((n, flat_rows, width), jnp.float32),
            VMEM((n, flat_rows, width), jnp.float32),
        ]
        + semaphores("pitch", 2),
        compiler_params=pltpu.CompilerParams(collective_id=0, has_side_effects=True),
        name="spectral",
    )(
        jnp.concatenate([turn_cos, turn_sin]),
        jnp.concatenate([planes, edges]),
        table,
        picked,
        factor,
    )
    edge_shape = (2,) + prior.shape[:-1]
    count = int(np.prod(edge_shape))

    def edges_of(device):
        piece = lax.dynamic_index_in_dim(gathered, device, 0, keepdims=False)
        return piece.reshape(-1)[:count].reshape(edge_shape)

    before = edges_of(lax.rem(me + n - 1, n))[1][..., None]
    after = edges_of(lax.rem(me + 1, n))[0][..., None]

    return correction.reshape(2, nv, rows, width), before, after


def body(residual, inverse_diagonal, prior, coupling, characteristic, cutoffs):
    nv, axial, rows, width = residual.shape
    cells = axial * width
    tile = (cells // LANES, LANES)
    n = lax.axis_size("span")

    def by_row(field):
        lead = field.shape[:-3]
        return jnp.moveaxis(field, -2, -3).reshape((-1, rows) + tile)

    diag = by_row(inverse_diagonal)
    correction, before, after = corrections(residual, prior, characteristic, cutoffs)
    corrected = by_row(residual.at[:, 0].add(correction[0]).at[:, -1].add(correction[1]))
    blank = jnp.zeros_like(prior[:, :1])
    neighbours = by_row(
        jnp.stack(
            [
                jnp.concatenate([before, prior[..., :-1]], axis=3),
                jnp.concatenate([prior[..., 1:], after], axis=3),
                jnp.concatenate([blank, prior[:, :-1]], axis=1),
                jnp.concatenate([prior[:, 1:], blank], axis=1),
            ]
        )
    )
    scalars = coupling.reshape(-1)
    nn = nv * nv
    count = 2 * nv + 3 * nn
    smem = pl.BlockSpec(memory_space=SMEM)
    vmem = pl.BlockSpec(memory_space=VMEM)
    share = cells // n
    update = pl.pallas_call(
        lambda *refs: sweeps_kernel(nv, *refs),
        out_shape=jax.ShapeDtypeStruct((nv, rows) + tile, jnp.float32),
        in_specs=[smem, vmem, vmem, vmem],
        out_specs=vmem,
        scratch_shapes=[
            VMEM((nv, rows) + tile, jnp.float32),
            VMEM((rows, nn) + tile, jnp.float32),
            VMEM((rows, nv) + tile, jnp.float32),
            VMEM((count,) + tile, jnp.float32),
            VMEM((n, count, share), jnp.float32),
            VMEM((n, count, share), jnp.float32),
            VMEM((n, 2 * nv, share), jnp.float32),
            VMEM((n, 2 * nv, share), jnp.float32),
            VMEM((2 * nv,) + tile, jnp.float32),
        ]
        + semaphores("span", 2),
        compiler_params=pltpu.CompilerParams(collective_id=1, has_side_effects=True),
        name="sweeps",
    )(scalars, diag, corrected, neighbours)
    return jnp.moveaxis(update.reshape(nv, rows, axial, width), 1, 2)


def solution(mesh):
    in_specs = (
        P(None, None, "span", "pitch"),
        P(None, None, None, "span", "pitch"),
        P(None, None, "span", "pitch"),
        P(),
        P(),
        P(),
    )
    out_specs = P(None, None, "span", "pitch")
    return jax.shard_map(body, mesh=mesh, in_specs=in_specs, out_specs=out_specs, check_vma=False)
```

```python
import jax
import jax.numpy as jnp
import numpy as np
from jax import lax
from jax.experimental import pallas as pl
from jax.experimental.pallas import tpu as pltpu
from jax.sharding import PartitionSpec as P

highest = lax.Precision.HIGHEST
LANES = 128
VMEM = pltpu.VMEM
SMEM = pltpu.SMEM


def greet(axis):
    n = lax.axis_size(axis)
    me = lax.axis_index(axis)
    barrier = pltpu.get_barrier_semaphore()
    for step in range(1, n):
        pl.semaphore_signal(
            barrier,
            inc=1,
            device_id={axis: lax.rem(me + step, n)},
            device_id_type=pl.DeviceIdType.MESH,
        )


def greeted(axis):
    pl.semaphore_wait(pltpu.get_barrier_semaphore(), lax.axis_size(axis) - 1)


def start_exchange(source, target, send, recv, axis, gather):
    n = lax.axis_size(axis)
    me = lax.axis_index(axis)
    copies = []
    for step in range(1, n):
        to = lax.rem(me + step, n)
        copy = pltpu.make_async_remote_copy(
            src_ref=source if gather else source.at[to],
            dst_ref=target.at[me],
            send_sem=send.at[step - 1],
            recv_sem=recv.at[step - 1],
            device_id={axis: to},
            device_id_type=pl.DeviceIdType.MESH,
        )
        copy.start()
        copies.append(copy)
    return copies


def wait_all(copies):
    for copy in copies:
        copy.wait()


def semaphores(axis, exchanges):
    n = lax.axis_size(axis)
    return [pltpu.SemaphoreType.DMA((n - 1,)) for _ in range(2 * exchanges)]


def total(terms):
    result = terms[0]
    for term in terms[1:]:
        result = result + term
    return result


def scaled(block, matrix, nv):
    return [
        [-total([block[i][j] * matrix(j, k) for j in range(nv)]) for k in range(nv)]
        for i in range(nv)
    ]


def times(block, vector, nv):
    return [total([block[i][j] * vector[j] for j in range(nv)]) for i in range(nv)]


def load_block(diag, row, nv):
    return [[diag[i * nv + j, row] for j in range(nv)] for i in range(nv)]


def local_kernel(nv, coupling, diag, residual, neighbours, source, packed, maps, stars):
    rows = diag.shape[1]
    tile = diag.shape[2:]
    zero = jnp.zeros(tile, jnp.float32)
    one = jnp.ones(tile, jnp.float32)

    def entry(which):
        return lambda i, j: coupling[(which * nv + i) * nv + j]

    identity = [zero + (one if i == j else zero) for j in range(nv) for i in range(nv)]

    def column(flat, j):
        return flat[j * nv:(j + 1) * nv]

    def forward(row, carry):
        star, grown = list(carry[:nv]), list(carry[nv:])
        block = load_block(diag, row, nv)
        rhs = []
        for i in range(nv):
            value = residual[i, row]
            for side in range(4):
                matrix = entry(2 + side)
                for j in range(nv):
                    value = value - matrix(i, j) * neighbours[side * nv + j, row]
            source[i, row] = value
            rhs.append(value)
        step = scaled(block, entry(0), nv)
        star = [x + y for x, y in zip(times(block, rhs, nv), times(step, star, nv))]
        new = []
        for j in range(nv):
            new += times(step, column(grown, j), nv)
        for i in range(nv):
            stars[row, i] = star[i]
        for m in range(nv * nv):
            maps[row, m] = new[m]
        return tuple(star + new)

    last = lax.fori_loop(0, rows, forward, tuple([zero] * nv + identity))
    for m in range(nv + nv * nv):
        packed[m] = last[m]

    def backward(index, carry):
        row = rows - 1 - index
        nn = nv * nv
        base, response, grown = list(carry[:nv]), list(carry[nv:nv + nn]), list(carry[nv + nn:])
        step = scaled(load_block(diag, row, nv), entry(1), nv)
        base = [stars[row, i] + y for i, y in enumerate(times(step, base, nv))]
        new_response, new = [], []
        for j in range(nv):
            moved = times(step, column(response, j), nv)
            new_response += [maps[row, j * nv + i] + moved[i] for i in range(nv)]
            new += times(step, column(grown, j), nv)
        return tuple(base + new_response + new)

    initial = tuple([zero] * (nv + nv * nv) + identity)
    final = lax.fori_loop(0, rows, backward, initial)
    for m in range(nv + 2 * nv * nv):
        packed[nv + nv * nv + m] = final[m]


def solve_kernel(nv, got, out):
    n = got.shape[0]
    lanes = got.shape[2]
    nn = nv * nv

    def mapped(d, start, vector):
        return total(
            [
                got[d, start + j * nv:start + (j + 1) * nv, :] * vector[j:j + 1]
                for j in range(nv)
            ]
        )

    incoming = jnp.zeros((nv, lanes), jnp.float32)
    all_incoming = []
    for d in range(n):
        all_incoming.append(incoming)
        out[d, 0:nv, :] = incoming
        if d + 1 < n:
            incoming = got[d, 0:nv, :] + mapped(d, nv, incoming)
    following = jnp.zeros((nv, lanes), jnp.float32)
    base = nv + nn
    for d in reversed(range(n)):
        out[d, nv:2 * nv, :] = following
        if d > 0:
            known = got[d, base:base + nv, :] + mapped(d, base + nv, all_incoming[d])
            following = known + mapped(d, base + nv + nn, following)


def final_kernel(nv, coupling, diag, source, incoming, update, stars):
    rows = diag.shape[1]

    def mixed(which, vector):
        return [
            total([coupling[(which * nv + i) * nv + j] * vector[j] for j in range(nv)])
            for i in range(nv)
        ]

    def forward(row, star):
        pushed = mixed(0, star)
        rhs = [source[i, row] - pushed[i] for i in range(nv)]
        star = times(load_block(diag, row, nv), rhs, nv)
        for i in range(nv):
            stars[row, i] = star[i]
        return tuple(star)

    lax.fori_loop(0, rows, forward, tuple(incoming[i] for i in range(nv)))

    def backward(index, following):
        row = rows - 1 - index
        moved = times(load_block(diag, row, nv), mixed(1, following), nv)
        value = [stars[row, i] - moved[i] for i in range(nv)]
        for i in range(nv):
            update[i, row] = value[i]
        return tuple(value)

    lax.fori_loop(0, rows, backward, tuple(incoming[nv + i] for i in range(nv)))


def spectral_kernel(
    nv, rows, turns, cutoffs, x_ref, all_tables, entries, out, edges,
    got, parts, landed, table, picked, fetched, s0, r0, s1, r1
):
    n = lax.axis_size("pitch")
    me = lax.axis_index("pitch")
    flat = 2 * nv * rows
    greet("pitch")
    fetch = pltpu.make_async_copy(all_tables.at[me], table, fetched)
    fetch.start()
    got[me] = x_ref[...]
    turn = [turns[part * n * n + me * n + q] for part in range(2) for q in range(n)]
    harmonics = entries.shape[1]
    own = harmonics // n
    points = n * x_ref.shape[1]
    chosen = lax.broadcasted_iota(jnp.int32, (harmonics, own), 0) == (
        n * lax.broadcasted_iota(jnp.int32, (harmonics, own), 1) + me
    )
    picked[...] = jnp.dot(
        entries[...],
        jnp.where(chosen, 1.0, 0.0).astype(jnp.float32),
        precision=highest,
        preferred_element_type=jnp.float32,
    )
    mine = n * lax.broadcasted_iota(jnp.int32, (1, own), 1) + me
    weights = jnp.where(mine == 0, 1.0, 2.0).astype(jnp.float32) / points
    greeted("pitch")
    wait_all(start_exchange(x_ref, got, s0, r0, "pitch", True))
    fetch.wait()
    edges[...] = got[:, flat:, :]
    waves = total([got[q, :flat, :] * turn[q] for q in range(n)])
    waves_imag = -total([got[q, :flat, :] * turn[n + q] for q in range(n)])
    both = jnp.concatenate([waves, waves_imag])
    cosine, sine = table[0], table[1]
    with_cos = jnp.dot(both, cosine, precision=highest, preferred_element_type=jnp.float32)
    with_sin = jnp.dot(both, sine, precision=highest, preferred_element_type=jnp.float32)
    real_part = with_cos[:flat] + with_sin[flat:]
    imag_part = with_cos[flat:] - with_sin[:flat]
    out_real, out_imag = [], []
    for q in range(2):
        weight = jnp.where(mine < cutoffs[q], weights, 0.0)
        sr = [real_part[(q * nv + j) * rows:(q * nv + j + 1) * rows] for j in range(nv)]
        si = [imag_part[(q * nv + j) * rows:(q * nv + j + 1) * rows] for j in range(nv)]
        for i in range(nv):
            at = [((i * nv + j) * 2 + q) * 2 for j in range(nv)]
            cr = [picked[m:m + 1, :] for m in at]
            ci = [picked[m + 1:m + 2, :] for m in at]
            out_real.append(total([cr[j] * sr[j] - ci[j] * si[j] for j in range(nv)]) * weight)
            out_imag.append(total([cr[j] * si[j] + ci[j] * sr[j] for j in range(nv)]) * weight)
    stacked = jnp.concatenate(out_real + out_imag)

    def back(matrix):
        return lax.dot_general(
            stacked,
            matrix,
            (((1,), (1,)), ((), ())),
            precision=highest,
            preferred_element_type=jnp.float32,
        )

    with_cos, with_sin = back(cosine), back(sine)
    field = with_cos[:flat] - with_sin[flat:]
    field_imag = with_sin[:flat] + with_cos[flat:]
    for q in range(n):
        parts[q] = field * turn[q] - field_imag * turn[n + q]
    copies = start_exchange(parts, landed, s1, r1, "pitch", False)
    landed[me] = parts[me]
    wait_all(copies)
    out[...] = total([landed[q] for q in range(n)])


def sweeps_kernel(
    nv, coupling, diag, residual, neighbours, update,
    source, maps, stars, packed, send, got, solved, back, incoming, s0, r0, s1, r1
):
    n = lax.axis_size("span")
    me = lax.axis_index("span")
    share = send.shape[2]
    pieces = LANES // share
    greet("span")
    local_kernel(nv, coupling, diag, residual, neighbours, source, packed, maps, stars)
    for m in range(packed.shape[0]):
        value = packed[m]
        if pieces == 1:
            send[:, m, :] = value
        else:
            for d in range(n):
                lane = d % pieces * share
                row = d // pieces
                send[d, m:m + 1, :] = value[row:row + 1, lane:lane + share]
    greeted("span")
    copies = start_exchange(send, got, s0, r0, "span", False)
    got[me] = send[me]
    wait_all(copies)
    solve_kernel(nv, got, solved)
    copies = start_exchange(solved, back, s1, r1, "span", False)
    back[me] = solved[me]
    wait_all(copies)
    for m in range(2 * nv):
        if pieces == 1:
            incoming[m] = back[:, m, :]
        else:
            for d in range(n):
                lane = d % pieces * share
                row = d // pieces
                incoming[m, row:row + 1, lane:lane + share] = back[d, m:m + 1, :]
    final_kernel(nv, coupling, diag, source, incoming, update, stars)


def tables(n, width, harmonics):
    points = n * width
    own = harmonics // n
    k = n * np.arange(own)[None, :] + np.arange(n)[:, None]
    product = (np.arange(width)[None, :, None] * k[:, None, :]) % points
    angle = product * (2.0 * np.pi / points)
    return np.stack([np.cos(angle), np.sin(angle)], axis=1).astype(np.float32)


def corrections(residual, prior, characteristic, cutoffs):
    n = lax.axis_size("pitch")
    me = lax.axis_index("pitch")
    nv, _, rows, width = residual.shape
    harmonics = characteristic.shape[2]
    points = n * width
    own = harmonics // n
    flat_rows = 2 * nv * rows
    planes = jnp.stack([residual[:, 0], residual[:, -1]]).reshape(flat_rows, width)
    edges = jnp.stack([prior[..., 0], prior[..., -1]]).reshape(-1)
    edge_rows = -(-edges.shape[0] // width)
    edge_rows = -(-edge_rows // 8) * 8
    edges = jnp.pad(edges, (0, edge_rows * width - edges.shape[0])).reshape(edge_rows, width)
    turn = 2.0 * np.pi * (np.arange(n)[:, None] * np.arange(n)[None, :] % n) / n
    turns = jnp.asarray(np.concatenate([np.cos(turn), np.sin(turn)]).reshape(-1), jnp.float32)
    entries = characteristic.transpose(3, 4, 0, 1, 2).reshape(-1, harmonics)
    smem = pl.BlockSpec(memory_space=SMEM)
    vmem = pl.BlockSpec(memory_space=VMEM)
    total_rows = flat_rows + edge_rows
    correction, gathered = pl.pallas_call(
        lambda *refs: spectral_kernel(nv, rows, *refs),
        out_shape=(
            jax.ShapeDtypeStruct((flat_rows, width), jnp.float32),
            jax.ShapeDtypeStruct((n, edge_rows, width), jnp.float32),
        ),
        in_specs=[smem, smem, vmem, pl.BlockSpec(memory_space=pl.ANY), vmem],
        out_specs=(vmem, vmem),
        scratch_shapes=[
            VMEM((n, total_rows, width), jnp.float32),
            VMEM((n, flat_rows, width), jnp.float32),
            VMEM((n, flat_rows, width), jnp.float32),
            VMEM((2, width, own), jnp.float32),
            VMEM((entries.shape[0], own), jnp.float32),
            pltpu.SemaphoreType.DMA,
        ]
        + semaphores("pitch", 2),
        compiler_params=pltpu.CompilerParams(collective_id=0, has_side_effects=True),
        name="spectral",
    )(
        turns,
        cutoffs,
        jnp.concatenate([planes, edges]),
        jnp.asarray(tables(n, width, harmonics)),
        entries,
    )
    edge_shape = (2,) + prior.shape[:-1]
    count = int(np.prod(edge_shape))

    def edges_of(device):
        piece = lax.dynamic_index_in_dim(gathered, device, 0, keepdims=False)
        return piece.reshape(-1)[:count].reshape(edge_shape)

    before = edges_of(lax.rem(me + n - 1, n))[1][..., None]
    after = edges_of(lax.rem(me + 1, n))[0][..., None]

    return correction.reshape(2, nv, rows, width), before, after


def body(residual, inverse_diagonal, prior, coupling, characteristic, cutoffs):
    nv, axial, rows, width = residual.shape
    cells = axial * width
    tile = (cells // LANES, LANES)
    n = lax.axis_size("span")

    def by_row(field):
        lead = field.shape[:-3]
        return jnp.moveaxis(field, -2, -3).reshape((-1, rows) + tile)

    diag = by_row(inverse_diagonal)
    correction, before, after = corrections(residual, prior, characteristic, cutoffs)
    corrected = by_row(residual.at[:, 0].add(correction[0]).at[:, -1].add(correction[1]))
    blank = jnp.zeros_like(prior[:, :1])
    neighbours = by_row(
        jnp.stack(
            [
                jnp.concatenate([before, prior[..., :-1]], axis=3),
                jnp.concatenate([prior[..., 1:], after], axis=3),
                jnp.concatenate([blank, prior[:, :-1]], axis=1),
                jnp.concatenate([prior[:, 1:], blank], axis=1),
            ]
        )
    )
    scalars = coupling.reshape(-1)
    nn = nv * nv
    count = 2 * nv + 3 * nn
    smem = pl.BlockSpec(memory_space=SMEM)
    vmem = pl.BlockSpec(memory_space=VMEM)
    share = cells // n
    update = pl.pallas_call(
        lambda *refs: sweeps_kernel(nv, *refs),
        out_shape=jax.ShapeDtypeStruct((nv, rows) + tile, jnp.float32),
        in_specs=[smem, vmem, vmem, vmem],
        out_specs=vmem,
        scratch_shapes=[
            VMEM((nv, rows) + tile, jnp.float32),
            VMEM((rows, nn) + tile, jnp.float32),
            VMEM((rows, nv) + tile, jnp.float32),
            VMEM((count,) + tile, jnp.float32),
            VMEM((n, count, share), jnp.float32),
            VMEM((n, count, share), jnp.float32),
            VMEM((n, 2 * nv, share), jnp.float32),
            VMEM((n, 2 * nv, share), jnp.float32),
            VMEM((2 * nv,) + tile, jnp.float32),
        ]
        + semaphores("span", 2),
        compiler_params=pltpu.CompilerParams(collective_id=1, has_side_effects=True),
        name="sweeps",
    )(scalars, diag, corrected, neighbours)
    return jnp.moveaxis(update.reshape(nv, rows, axial, width), 1, 2)


def solution(mesh):
    in_specs = (
        P(None, None, "span", "pitch"),
        P(None, None, None, "span", "pitch"),
        P(None, None, "span", "pitch"),
        P(),
        P(),
        P(),
    )
    out_specs = P(None, None, "span", "pitch")
    return jax.shard_map(body, mesh=mesh, in_specs=in_specs, out_specs=out_specs, check_vma=False)
```

```python
import jax
import jax.numpy as jnp
import numpy as np
from jax import lax
from jax.experimental import pallas as pl
from jax.experimental.pallas import tpu as pltpu
from jax.sharding import PartitionSpec as P

highest = lax.Precision.HIGHEST
LANES = 128
VMEM = pltpu.VMEM
SMEM = pltpu.SMEM


def greet(axis):
    n = lax.axis_size(axis)
    me = lax.axis_index(axis)
    barrier = pltpu.get_barrier_semaphore()
    for step in range(1, n):
        pl.semaphore_signal(
            barrier,
            inc=1,
            device_id={axis: lax.rem(me + step, n)},
            device_id_type=pl.DeviceIdType.MESH,
        )


def greeted(axis):
    pl.semaphore_wait(pltpu.get_barrier_semaphore(), lax.axis_size(axis) - 1)


def start_exchange(source, target, send, recv, axis, gather):
    n = lax.axis_size(axis)
    me = lax.axis_index(axis)
    copies = []
    for step in sorted(range(1, n), key=lambda step: -min(step, n - step)):
        to = lax.rem(me + step, n)
        copy = pltpu.make_async_remote_copy(
            src_ref=source if gather else source.at[to],
            dst_ref=target.at[me],
            send_sem=send.at[step - 1],
            recv_sem=recv.at[step - 1],
            device_id={axis: to},
            device_id_type=pl.DeviceIdType.MESH,
        )
        copy.start()
        copies.append(copy)
    return copies


def wait_all(copies):
    for copy in copies:
        copy.wait()


def semaphores(axis, exchanges):
    n = lax.axis_size(axis)
    return [pltpu.SemaphoreType.DMA((n - 1,)) for _ in range(2 * exchanges)]


def total(terms):
    result = terms[0]
    for term in terms[1:]:
        result = result + term
    return result


def scaled(block, matrix, nv):
    return [
        [-total([block[i][j] * matrix(j, k) for j in range(nv)]) for k in range(nv)]
        for i in range(nv)
    ]


def times(block, vector, nv):
    return [total([block[i][j] * vector[j] for j in range(nv)]) for i in range(nv)]


def load_block(diag, row, nv):
    return [[diag[i * nv + j, row] for j in range(nv)] for i in range(nv)]


def local_kernel(nv, coupling, diag, residual, neighbours, source, packed, maps, stars):
    rows = diag.shape[1]
    tile = diag.shape[2:]
    zero = jnp.zeros(tile, jnp.float32)
    one = jnp.ones(tile, jnp.float32)

    def entry(which):
        return lambda i, j: coupling[(which * nv + i) * nv + j]

    identity = [zero + (one if i == j else zero) for j in range(nv) for i in range(nv)]

    def column(flat, j):
        return flat[j * nv:(j + 1) * nv]

    def forward(row, carry):
        star, grown = list(carry[:nv]), list(carry[nv:])
        block = load_block(diag, row, nv)
        rhs = []
        for i in range(nv):
            value = residual[i, row]
            for side in range(4):
                matrix = entry(2 + side)
                for j in range(nv):
                    value = value - matrix(i, j) * neighbours[side * nv + j, row]
            source[i, row] = value
            rhs.append(value)
        step = scaled(block, entry(0), nv)
        star = [x + y for x, y in zip(times(block, rhs, nv), times(step, star, nv))]
        new = []
        for j in range(nv):
            new += times(step, column(grown, j), nv)
        for i in range(nv):
            stars[row, i] = star[i]
        for m in range(nv * nv):
            maps[row, m] = new[m]
        return tuple(star + new)

    last = lax.fori_loop(0, rows, forward, tuple([zero] * nv + identity))
    for m in range(nv + nv * nv):
        packed[m] = last[m]

    def backward(index, carry):
        row = rows - 1 - index
        nn = nv * nv
        base, response, grown = list(carry[:nv]), list(carry[nv:nv + nn]), list(carry[nv + nn:])
        step = scaled(load_block(diag, row, nv), entry(1), nv)
        base = [stars[row, i] + y for i, y in enumerate(times(step, base, nv))]
        new_response, new = [], []
        for j in range(nv):
            moved = times(step, column(response, j), nv)
            new_response += [maps[row, j * nv + i] + moved[i] for i in range(nv)]
            new += times(step, column(grown, j), nv)
        return tuple(base + new_response + new)

    initial = tuple([zero] * (nv + nv * nv) + identity)
    final = lax.fori_loop(0, rows, backward, initial)
    for m in range(nv + 2 * nv * nv):
        packed[nv + nv * nv + m] = final[m]


def solve_kernel(nv, got, out):
    n = got.shape[0]
    lanes = got.shape[2]
    nn = nv * nv

    def mapped(d, start, vector):
        return total(
            [
                got[d, start + j * nv:start + (j + 1) * nv, :] * vector[j:j + 1]
                for j in range(nv)
            ]
        )

    incoming = jnp.zeros((nv, lanes), jnp.float32)
    all_incoming = []
    for d in range(n):
        all_incoming.append(incoming)
        out[d, 0:nv, :] = incoming
        if d + 1 < n:
            incoming = got[d, 0:nv, :] + mapped(d, nv, incoming)
    following = jnp.zeros((nv, lanes), jnp.float32)
    base = nv + nn
    for d in reversed(range(n)):
        out[d, nv:2 * nv, :] = following
        if d > 0:
            known = got[d, base:base + nv, :] + mapped(d, base + nv, all_incoming[d])
            following = known + mapped(d, base + nv + nn, following)


def final_kernel(nv, coupling, diag, source, incoming, update, stars):
    rows = diag.shape[1]

    def mixed(which, vector):
        return [
            total([coupling[(which * nv + i) * nv + j] * vector[j] for j in range(nv)])
            for i in range(nv)
        ]

    def forward(row, star):
        pushed = mixed(0, star)
        rhs = [source[i, row] - pushed[i] for i in range(nv)]
        star = times(load_block(diag, row, nv), rhs, nv)
        for i in range(nv):
            stars[row, i] = star[i]
        return tuple(star)

    lax.fori_loop(0, rows, forward, tuple(incoming[i] for i in range(nv)))

    def backward(index, following):
        row = rows - 1 - index
        moved = times(load_block(diag, row, nv), mixed(1, following), nv)
        value = [stars[row, i] - moved[i] for i in range(nv)]
        for i in range(nv):
            update[i, row] = value[i]
        return tuple(value)

    lax.fori_loop(0, rows, backward, tuple(incoming[nv + i] for i in range(nv)))


def spectral_kernel(
    nv, rows, turns, cutoffs, x_ref, all_tables, entries, out, edges,
    got, parts, landed, table, picked, fetched, s0, r0, s1, r1
):
    n = lax.axis_size("pitch")
    me = lax.axis_index("pitch")
    flat = 2 * nv * rows
    greet("pitch")
    fetch = pltpu.make_async_copy(all_tables.at[me], table, fetched)
    fetch.start()
    got[me] = x_ref[...]
    turn = [turns[part * n * n + me * n + q] for part in range(2) for q in range(n)]
    harmonics = entries.shape[1]
    own = harmonics // n
    points = n * x_ref.shape[1]
    chosen = lax.broadcasted_iota(jnp.int32, (harmonics, own), 0) == (
        n * lax.broadcasted_iota(jnp.int32, (harmonics, own), 1) + me
    )
    picked[...] = jnp.dot(
        entries[...],
        jnp.where(chosen, 1.0, 0.0).astype(jnp.float32),
        precision=highest,
        preferred_element_type=jnp.float32,
    )
    mine = n * lax.broadcasted_iota(jnp.int32, (1, own), 1) + me
    weights = jnp.where(mine == 0, 1.0, 2.0).astype(jnp.float32) / points
    greeted("pitch")
    wait_all(start_exchange(x_ref, got, s0, r0, "pitch", True))
    fetch.wait()
    edges[...] = got[:, flat:, :]
    waves = total([got[q, :flat, :] * turn[q] for q in range(n)])
    waves_imag = -total([got[q, :flat, :] * turn[n + q] for q in range(n)])
    both = jnp.concatenate([waves, waves_imag])
    cosine, sine = table[0], table[1]
    with_cos = jnp.dot(both, cosine, precision=highest, preferred_element_type=jnp.float32)
    with_sin = jnp.dot(both, sine, precision=highest, preferred_element_type=jnp.float32)
    real_part = with_cos[:flat] + with_sin[flat:]
    imag_part = with_cos[flat:] - with_sin[:flat]
    out_real, out_imag = [], []
    for q in range(2):
        weight = jnp.where(mine < cutoffs[q], weights, 0.0)
        sr = [real_part[(q * nv + j) * rows:(q * nv + j + 1) * rows] for j in range(nv)]
        si = [imag_part[(q * nv + j) * rows:(q * nv + j + 1) * rows] for j in range(nv)]
        for i in range(nv):
            at = [((i * nv + j) * 2 + q) * 2 for j in range(nv)]
            cr = [picked[m:m + 1, :] for m in at]
            ci = [picked[m + 1:m + 2, :] for m in at]
            out_real.append(total([cr[j] * sr[j] - ci[j] * si[j] for j in range(nv)]) * weight)
            out_imag.append(total([cr[j] * si[j] + ci[j] * sr[j] for j in range(nv)]) * weight)
    stacked = jnp.concatenate(out_real + out_imag)

    def back(matrix):
        return lax.dot_general(
            stacked,
            matrix,
            (((1,), (1,)), ((), ())),
            precision=highest,
            preferred_element_type=jnp.float32,
        )

    with_cos, with_sin = back(cosine), back(sine)
    field = with_cos[:flat] - with_sin[flat:]
    field_imag = with_sin[:flat] + with_cos[flat:]
    for q in range(n):
        parts[q] = field * turn[q] - field_imag * turn[n + q]
    copies = start_exchange(parts, landed, s1, r1, "pitch", False)
    landed[me] = parts[me]
    wait_all(copies)
    out[...] = total([landed[q] for q in range(n)])


def sweeps_kernel(
    nv, coupling, diag, residual, neighbours, update,
    source, maps, stars, packed, send, got, solved, back, incoming, s0, r0, s1, r1
):
    n = lax.axis_size("span")
    me = lax.axis_index("span")
    share = send.shape[2]
    pieces = LANES // share
    greet("span")
    local_kernel(nv, coupling, diag, residual, neighbours, source, packed, maps, stars)
    for m in range(packed.shape[0]):
        value = packed[m]
        if pieces == 1:
            send[:, m, :] = value
        else:
            for d in range(n):
                lane = d % pieces * share
                row = d // pieces
                send[d, m:m + 1, :] = value[row:row + 1, lane:lane + share]
    greeted("span")
    copies = start_exchange(send, got, s0, r0, "span", False)
    got[me] = send[me]
    wait_all(copies)
    solve_kernel(nv, got, solved)
    copies = start_exchange(solved, back, s1, r1, "span", False)
    back[me] = solved[me]
    wait_all(copies)
    for m in range(2 * nv):
        if pieces == 1:
            incoming[m] = back[:, m, :]
        else:
            for d in range(n):
                lane = d % pieces * share
                row = d // pieces
                incoming[m, row:row + 1, lane:lane + share] = back[d, m:m + 1, :]
    final_kernel(nv, coupling, diag, source, incoming, update, stars)


def tables(n, width, harmonics):
    points = n * width
    own = harmonics // n
    k = n * np.arange(own)[None, :] + np.arange(n)[:, None]
    product = (np.arange(width)[None, :, None] * k[:, None, :]) % points
    angle = product * (2.0 * np.pi / points)
    return np.stack([np.cos(angle), np.sin(angle)], axis=1).astype(np.float32)


def corrections(residual, prior, characteristic, cutoffs):
    n = lax.axis_size("pitch")
    me = lax.axis_index("pitch")
    nv, _, rows, width = residual.shape
    harmonics = characteristic.shape[2]
    points = n * width
    own = harmonics // n
    flat_rows = 2 * nv * rows
    planes = jnp.stack([residual[:, 0], residual[:, -1]]).reshape(flat_rows, width)
    edges = jnp.stack([prior[..., 0], prior[..., -1]]).reshape(-1)
    edge_rows = -(-edges.shape[0] // width)
    edge_rows = -(-edge_rows // 8) * 8
    edges = jnp.pad(edges, (0, edge_rows * width - edges.shape[0])).reshape(edge_rows, width)
    turn = 2.0 * np.pi * (np.arange(n)[:, None] * np.arange(n)[None, :] % n) / n
    turns = jnp.asarray(np.concatenate([np.cos(turn), np.sin(turn)]).reshape(-1), jnp.float32)
    entries = characteristic.transpose(3, 4, 0, 1, 2).reshape(-1, harmonics)
    smem = pl.BlockSpec(memory_space=SMEM)
    vmem = pl.BlockSpec(memory_space=VMEM)
    total_rows = flat_rows + edge_rows
    correction, gathered = pl.pallas_call(
        lambda *refs: spectral_kernel(nv, rows, *refs),
        out_shape=(
            jax.ShapeDtypeStruct((flat_rows, width), jnp.float32),
            jax.ShapeDtypeStruct((n, edge_rows, width), jnp.float32),
        ),
        in_specs=[smem, smem, vmem, pl.BlockSpec(memory_space=pl.ANY), vmem],
        out_specs=(vmem, vmem),
        scratch_shapes=[
            VMEM((n, total_rows, width), jnp.float32),
            VMEM((n, flat_rows, width), jnp.float32),
            VMEM((n, flat_rows, width), jnp.float32),
            VMEM((2, width, own), jnp.float32),
            VMEM((entries.shape[0], own), jnp.float32),
            pltpu.SemaphoreType.DMA,
        ]
        + semaphores("pitch", 2),
        compiler_params=pltpu.CompilerParams(collective_id=0, has_side_effects=True),
        name="spectral",
    )(
        turns,
        cutoffs,
        jnp.concatenate([planes, edges]),
        jnp.asarray(tables(n, width, harmonics)),
        entries,
    )
    edge_shape = (2,) + prior.shape[:-1]
    count = int(np.prod(edge_shape))

    def edges_of(device):
        piece = lax.dynamic_index_in_dim(gathered, device, 0, keepdims=False)
        return piece.reshape(-1)[:count].reshape(edge_shape)

    before = edges_of(lax.rem(me + n - 1, n))[1][..., None]
    after = edges_of(lax.rem(me + 1, n))[0][..., None]

    return correction.reshape(2, nv, rows, width), before, after


def body(residual, inverse_diagonal, prior, coupling, characteristic, cutoffs):
    nv, axial, rows, width = residual.shape
    cells = axial * width
    tile = (cells // LANES, LANES)
    n = lax.axis_size("span")

    def by_row(field):
        lead = field.shape[:-3]
        return jnp.moveaxis(field, -2, -3).reshape((-1, rows) + tile)

    diag = by_row(inverse_diagonal)
    correction, before, after = corrections(residual, prior, characteristic, cutoffs)
    corrected = by_row(residual.at[:, 0].add(correction[0]).at[:, -1].add(correction[1]))
    blank = jnp.zeros_like(prior[:, :1])
    neighbours = by_row(
        jnp.stack(
            [
                jnp.concatenate([before, prior[..., :-1]], axis=3),
                jnp.concatenate([prior[..., 1:], after], axis=3),
                jnp.concatenate([blank, prior[:, :-1]], axis=1),
                jnp.concatenate([prior[:, 1:], blank], axis=1),
            ]
        )
    )
    scalars = coupling.reshape(-1)
    nn = nv * nv
    count = 2 * nv + 3 * nn
    smem = pl.BlockSpec(memory_space=SMEM)
    vmem = pl.BlockSpec(memory_space=VMEM)
    share = cells // n
    update = pl.pallas_call(
        lambda *refs: sweeps_kernel(nv, *refs),
        out_shape=jax.ShapeDtypeStruct((nv, rows) + tile, jnp.float32),
        in_specs=[smem, vmem, vmem, vmem],
        out_specs=vmem,
        scratch_shapes=[
            VMEM((nv, rows) + tile, jnp.float32),
            VMEM((rows, nn) + tile, jnp.float32),
            VMEM((rows, nv) + tile, jnp.float32),
            VMEM((count,) + tile, jnp.float32),
            VMEM((n, count, share), jnp.float32),
            VMEM((n, count, share), jnp.float32),
            VMEM((n, 2 * nv, share), jnp.float32),
            VMEM((n, 2 * nv, share), jnp.float32),
            VMEM((2 * nv,) + tile, jnp.float32),
        ]
        + semaphores("span", 2),
        compiler_params=pltpu.CompilerParams(collective_id=1, has_side_effects=True),
        name="sweeps",
    )(scalars, diag, corrected, neighbours)
    return jnp.moveaxis(update.reshape(nv, rows, axial, width), 1, 2)


def solution(mesh):
    in_specs = (
        P(None, None, "span", "pitch"),
        P(None, None, None, "span", "pitch"),
        P(None, None, "span", "pitch"),
        P(),
        P(),
        P(),
    )
    out_specs = P(None, None, "span", "pitch")
    return jax.shard_map(body, mesh=mesh, in_specs=in_specs, out_specs=out_specs, check_vma=False)
```
